32 devices in a mesh: lat: 8 (over z, x), lon: 4 (over y, core).
Axes of the slice: x: 2, y: 2, z: 4, core: 2. Of those that a mesh axis runs over, the one named last changes fastest.
Arguments:
- parent: bfloat16 [128, 128, 512], P('lat', 'lon'), may hold values from -6 to 6
- diffusion: float32 [512], replicated, may hold values from 0.05 to 0.25
- nest_state: bfloat16 [8192, 8, 512], P(('lat', 'lon')), may hold values from -6 to 6
- nest_cotangent: bfloat16 [8192, 8, 512], P(('lat', 'lon')), may hold values from -6 to 6
- owner_count: int32 [32], P(('lat', 'lon')), may hold values from 0 to 256, as said below
- tile_pos: int32 [8192], P(('lat', 'lon')), may hold values from 0 to 511
- w_in: bfloat16 [512, 2048], replicated, may hold values from -0.25 to 0.25
- w_out: bfloat16 [2048, 512], replicated, may hold values from -0.125 to 0.125
Outputs:
- parent_out: bfloat16 [128, 128, 512], P('lat', 'lon')
- nest_grad: bfloat16 [8192, 8, 512], P(('lat', 'lon'))
- w_in_grad: float32 [512, 2048], replicated
- w_out_grad: float32 [2048, 512], replicated
The draws below stay inside these ranges and needn't reach their ends.
Inputs may be any that keep to these rules, and one draw needn't show every extreme that they name: `owner_count`: the counts of all devices sum to 2048; each is a multiple of 8; some device has exactly 256. Only the first count slots of a device are live; the entries of its other slots are not used.
All inputs are finite; a program needn't handle non-finite values.
Results may differ from the reference program's by a relative error of at most 0.012.
Values may be sent and summed in bfloat16 or wider, within the bound.
No kernel may reach another device: no remote copies, remote signals or barrier semaphores. Data moves between devices by JAX's collectives and lax.ppermute only.
A program may use at most 128 MiB of HBM per device.

```python
import math
import jax
import jax.numpy as jnp
from jax import lax

C = 512
FF = 2048
BLAT = 16
BLON = 32
TILE_ROWS = 8
OWN = 256
NLAT = 128
NLON = 128
TILES = 8192
LIVE_TILES = 2048
CAP = 8
N_LON = 4


def draw_owner_count(key, part):
    devices = TILES // OWN
    half = OWN // 2
    steps_max = half // CAP
    pairs = devices // 4
    key_order = jax.random.fold_in(key, 11)
    key_extra = jax.random.fold_in(key, 23)
    order = jax.random.permutation(key_order, devices)
    extra = jax.random.randint(key_extra, (pairs,), 0, steps_max + 1)
    extra = extra.at[0].set(steps_max)
    first = half + CAP * extra
    second = half - CAP * extra
    values = jnp.concatenate([first, second, jnp.zeros((devices - 2 * pairs,), jnp.int32)]).astype(jnp.int32)
    return jnp.zeros((devices,), jnp.int32).at[order].set(values)


def with_ends(values, stream_key, smallest, largest):
    longest = values.shape.index(max(values.shape))
    spots = []
    for shift in (0, 1):
        where = [jax.random.randint(jax.random.fold_in(stream_key, axis), (), 0, length) for axis, length in enumerate(values.shape)]
        where[longest] = (where[longest] + shift) % values.shape[longest]
        spots.append(tuple(where))
    return values.at[spots[0]].set(smallest).at[spots[1]].set(largest)


def shard_levels(key, shape, split, smallest, high):
    def one(position, blocks):
        steps = jax.random.uniform(jax.random.fold_in(jax.random.fold_in(key, 6), position), (blocks,), jnp.float32, smallest / len(split), high / len(split))
        return jnp.repeat(jnp.exp(steps), shape[position] // blocks).reshape((-1,) + (1,) * (len(shape) - position - 1))

    level = one(*split[0])
    for cut in split[1:]:
        level = level * one(*cut)
    return level


def scatter_about(key, shape, deviation, limit, cuts=(), kind=jnp.bfloat16):
    loudness = shard_levels(key, shape, cuts, -0.22, 0.18) if cuts else 1.0
    drawn = jax.random.normal(key, shape, jnp.float32) * deviation * loudness
    return jnp.minimum(jnp.maximum(drawn, -limit), limit).astype(kind)


def setup_inputs(seed: int = 0) -> dict:
    seeds = jax.random.split(jax.random.key(seed), 9)
    return {
        "parent": scatter_about(seeds[0], (NLAT, NLON, C), 1.0, 6.0, ((0, 8), (1, 4))),
        "diffusion": jnp.clip(jnp.exp(jax.random.uniform(seeds[1], (C,), jnp.float32, math.log(0.05), math.log(0.25))), 0.05, 0.25),
        "nest_state": scatter_about(seeds[2], (TILES, TILE_ROWS, C), 1.0, 6.0, ((0, 32),)),
        "nest_cotangent": scatter_about(seeds[3], (TILES, TILE_ROWS, C), 1.0, 6.0, ((0, 32),)),
        "owner_count": draw_owner_count(jax.random.fold_in(seeds[8], 71), 0),
        "tile_pos": with_ends(jax.random.randint(seeds[5], (TILES,), 0, BLAT * BLON), jax.random.fold_in(seeds[5], 1), 0, (BLAT * BLON) - 1).astype(jnp.int32),
        "w_in": scatter_about(seeds[6], (C, FF), C ** -0.5, 0.25),
        "w_out": scatter_about(seeds[7], (FF, C), FF ** -0.5, 0.125),
    }


def nest_block(inputs, cotangent, w_in, w_out):
    count, cells, chans = inputs.shape
    rows = inputs.reshape(count * cells, chans)
    grads = cotangent.reshape(count * cells, chans)
    hidden = jnp.dot(rows, w_in, preferred_element_type=jnp.float32)
    active = jax.nn.gelu(hidden).astype(jnp.bfloat16)
    output = rows.astype(jnp.float32) + jnp.dot(active, w_out, preferred_element_type=jnp.float32)
    feedback = lax.optimization_barrier(jnp.mean(output.reshape(count, cells, chans), axis=1)).astype(jnp.bfloat16)
    d_active = jnp.dot(grads, w_out.T, preferred_element_type=jnp.float32)
    d_hidden = jax.vjp(jax.nn.gelu, hidden)[1](d_active)[0].astype(jnp.bfloat16)
    d_inputs = (grads.astype(jnp.float32) + jnp.dot(d_hidden, w_in.T, preferred_element_type=jnp.float32)).astype(jnp.bfloat16)
    grad_in = jnp.dot(rows.T, d_hidden, preferred_element_type=jnp.float32)
    grad_out = jnp.dot(active.T, grads, preferred_element_type=jnp.float32)
    return (d_inputs.reshape(count, cells, chans), feedback, grad_in, grad_out)

def reference(parent, diffusion, nest_state, nest_cotangent, owner_count, tile_pos, w_in, w_out):
    field = parent.astype(jnp.float32)
    lat_pad = jnp.pad(field, ((1, 1), (0, 0), (0, 0)))
    beside_all = lat_pad[2:] + lat_pad[:-2] + jnp.roll(field, 1, axis=1) + jnp.roll(field, -1, axis=1) - 4.0 * field
    smoothed = field + diffusion * beside_all
    slots = jnp.arange(TILES, dtype=jnp.int32)
    owner = (slots // OWN).astype(jnp.int32)
    local = (slots % OWN).astype(jnp.int32)
    live = local < owner_count[owner]
    lat_index = (owner // N_LON * BLAT + tile_pos // BLON).astype(jnp.int32)
    lon_index = (owner % N_LON * BLON + tile_pos % BLON).astype(jnp.int32)
    chosen = jnp.nonzero(live, size=LIVE_TILES)[0].astype(jnp.int32)
    group = 64
    blocks = chosen.reshape(LIVE_TILES // group, group)

    def one_block(carry, ids):
        context = smoothed[lat_index[ids], lon_index[ids]]
        inputs = (nest_state[ids].astype(jnp.float32) + context[:, None, :]).astype(jnp.bfloat16)
        d_inputs, feedback, grad_in, grad_out = nest_block(inputs, nest_cotangent[ids], w_in, w_out)
        return ((carry[0] + grad_in, carry[1] + grad_out), (d_inputs, feedback))
    start = (jnp.zeros((C, FF), jnp.float32), jnp.zeros((FF, C), jnp.float32))
    sums, stacked = lax.scan(one_block, start, blocks)
    d_inputs = stacked[0].reshape(LIVE_TILES, TILE_ROWS, C)
    feedback = stacked[1].reshape(LIVE_TILES, C).astype(jnp.float32)
    nest_grad = jnp.zeros((TILES, TILE_ROWS, C), jnp.bfloat16).at[chosen].set(d_inputs)
    summed = jnp.zeros((NLAT, NLON, C), jnp.float32).at[lat_index[chosen], lon_index[chosen]].add(feedback)
    parent_out = (smoothed + summed).astype(jnp.bfloat16)
    factor = 1.0 / math.sqrt(LIVE_TILES * TILE_ROWS)
    return (parent_out, nest_grad, sums[0] * factor, sums[1] * factor)
```

```python
import functools
import math

import jax
import jax.numpy as jnp
from jax import lax
from jax.experimental import pallas as pl
from jax.experimental.pallas import tpu as pltpu
from jax.sharding import PartitionSpec as P

AXES = ("lat", "lon")
BLOCK = 256
GELU_A = math.sqrt(2.0 / math.pi)
GELU_B = GELU_A * 0.044715


def halo(x, axis, dim, wrap):
    size, length = (lax.axis_size(axis), x.shape[dim])
    up = [(i, (i + 1) % size) for i in range(size if wrap else size - 1)]
    down = [(j, i) for i, j in up]
    last = lax.slice_in_dim(x, length - 1, length, axis=dim)
    first = lax.slice_in_dim(x, 0, 1, axis=dim)
    return lax.ppermute(last, axis, up), lax.ppermute(first, axis, down)


def nn(a, b):
    return lax.dot_general(a, b, (((1,), (0,)), ((), ())), preferred_element_type=jnp.float32)


def nt(a, b):
    return lax.dot_general(a, b, (((1,), (1,)), ((), ())), preferred_element_type=jnp.float32)


def tn(a, b):
    return lax.dot_general(a, b, (((0,), (0,)), ((), ())), preferred_element_type=jnp.float32)


def nest_kernel(factor, group, cells, x_ref, g_ref, win_ref, wout_ref, p_ref, dh_ref, mean_ref, act_ref, row_ref):
    rows, chans = x_ref.shape
    width = win_ref.shape[1]
    tiles = group // cells
    for i in range(rows // group):
        span = pl.ds(i * group, group)
        hidden = nn(x_ref[span, :], win_ref[...])
        d_act = nt(g_ref[span, :], wout_ref[...])
        square = hidden * hidden
        tanh = jnp.tanh(hidden * (GELU_A + GELU_B * square))
        cdf = 0.5 + 0.5 * tanh
        act = hidden * cdf
        slope = cdf + act * (1.0 - tanh) * (GELU_A + 3.0 * GELU_B * square)
        dh_ref[span, :] = (d_act * slope).astype(jnp.bfloat16)
        rounded = act.astype(jnp.bfloat16)
        act_ref[span, :] = rounded
        wide = rounded.astype(jnp.float32)
        for l in range(width // 128):
            lanes = slice(l * 128, (l + 1) * 128)
            row_ref[i % 2, l, :, :] = wide[:, lanes]
            total = row_ref[i % 2, l, pl.ds(0, tiles, stride=cells), :]
            for r in range(1, cells):
                total = total + row_ref[i % 2, l, pl.ds(r, tiles, stride=cells), :]
            mean_ref[pl.ds(i * tiles, tiles), lanes] = (total * (1.0 / cells)).astype(jnp.bfloat16)
    out = tn(act_ref[...], g_ref[...]) * factor
    for s in range(chans // width):
        p_ref[chans + s * width : chans + (s + 1) * width, :] = out[:, s * width : (s + 1) * width].astype(jnp.bfloat16)
    p_ref[:chans, :] = (tn(x_ref[...], dh_ref[...]) * factor).astype(jnp.bfloat16)


def nest_chunk(x, g, w_in, w_out, first, blocks, factor, cells):
    rows, chans = x.shape
    tiles = rows // cells
    group = min(256, rows)
    return pl.pallas_call(
        functools.partial(nest_kernel, factor, group, cells),
        grid=(blocks,),
        in_specs=[
            pl.BlockSpec(memory_space=pltpu.VMEM),
            pl.BlockSpec(memory_space=pltpu.VMEM),
            pl.BlockSpec((chans, BLOCK), lambda j: (0, first + j)),
            pl.BlockSpec((BLOCK, chans), lambda j: (first + j, 0)),
        ],
        out_specs=[
            pl.BlockSpec((2 * chans, BLOCK), lambda j: (j, 0)),
            pl.BlockSpec((rows, BLOCK), lambda j: (0, j)),
            pl.BlockSpec((tiles, BLOCK), lambda j: (0, j)),
        ],
        out_shape=[
            jax.ShapeDtypeStruct((blocks * 2 * chans, BLOCK), jnp.bfloat16),
            jax.ShapeDtypeStruct((rows, blocks * BLOCK), jnp.bfloat16),
            jax.ShapeDtypeStruct((tiles, blocks * BLOCK), jnp.bfloat16),
        ],
        scratch_shapes=[
            pltpu.VMEM((rows, BLOCK), jnp.bfloat16),
            pltpu.VMEM((2, BLOCK // 128, group, 128), jnp.float32),
        ],
        compiler_params=pltpu.CompilerParams(dimension_semantics=("arbitrary",), vmem_limit_bytes=32 << 20),
        cost_estimate=pl.CostEstimate(
            flops=8 * rows * chans * BLOCK * blocks,
            transcendentals=rows * BLOCK * blocks,
            bytes_accessed=4 * rows * chans + 2 * rows * BLOCK * blocks + 8 * chans * BLOCK * blocks,
        ),
        name="nest_chunk",
    )(x, g, w_in, w_out)


def widen_kernel(p_ref, *refs):
    gin_ref, gout_ref = refs[-2:]
    chans, width = gin_ref.shape
    gin_ref[...] = p_ref[:chans, :].astype(jnp.float32)
    for s in range(chans // width):
        gout_ref[:, s * width : (s + 1) * width] = p_ref[chans + s * width : chans + (s + 1) * width, :].astype(jnp.float32)


def widen(p, into, first, chans, hidden):
    blocks = p.shape[0] // (2 * chans)
    return pl.pallas_call(
        widen_kernel,
        grid=(blocks,),
        in_specs=[pl.BlockSpec((2 * chans, BLOCK), lambda j: (j, 0))] + [pl.BlockSpec(memory_space=pl.ANY)] * len(into),
        out_specs=[
            pl.BlockSpec((chans, BLOCK), lambda j: (0, first + j)),
            pl.BlockSpec((BLOCK, chans), lambda j: (first + j, 0)),
        ],
        out_shape=[
            jax.ShapeDtypeStruct((chans, hidden), jnp.float32),
            jax.ShapeDtypeStruct((hidden, chans), jnp.float32),
        ],
        input_output_aliases={1 + i: i for i in range(len(into))},
        cost_estimate=pl.CostEstimate(flops=0, transcendentals=0, bytes_accessed=12 * chans * BLOCK * blocks),
        name="widen",
    )(p, *into)


def add(a, b):
    return (a.astype(jnp.float32) + b.astype(jnp.float32)).astype(jnp.bfloat16)


def sum_steps(nlat, nlon):
    devices = nlat * nlon
    lon_bits = [1 << b for b in range(nlon.bit_length() - 1)]
    lat_bits = [nlon << b for b in range(nlat.bit_length() - 1)]
    core, near_lon, near_lat = lon_bits[0], lon_bits[1], lat_bits[0]
    head = [(core, core), (near_lat, near_lon), (near_lon, near_lat)]
    tail = [(m, m) for m in lon_bits[2:] + lat_bits[1:]]

    def pairs(masks):
        return [(i, i ^ (masks[1] if i & core else masks[0])) for i in range(devices)]

    def bit(masks):
        me = lax.axis_index(AXES)
        mask = jnp.where((me & core) != 0, masks[1], masks[0])
        return jnp.where((me & mask) != 0, 1, 0)

    def halve(masks, cur):
        half, mine = cur.shape[0] // 2, bit(masks)
        other = lax.dynamic_slice_in_dim(cur, (1 - mine) * half, half, 0)
        kept = lax.dynamic_slice_in_dim(cur, mine * half, half, 0)
        return add(kept, lax.ppermute(other, AXES, pairs(masks)))

    def both(masks, cur):
        return add(cur, lax.ppermute(cur, AXES, pairs(masks)))

    def double(masks, cur):
        got = lax.ppermute(cur, AXES, pairs(masks))
        return jnp.where(bit(masks) == 1, jnp.concatenate([got, cur]), jnp.concatenate([cur, got]))

    halved = head + tail[:-1]
    steps = [functools.partial(halve, m) for m in halved]
    steps += [functools.partial(both, m) for m in tail[-1:]]
    steps += [functools.partial(double, m) for m in reversed(halved)]
    return steps


def local(parent, diffusion, nest_state, nest_cotangent, owner_count, tile_pos, w_in, w_out):
    blat, blon, chans = parent.shape
    own, cells = (nest_state.shape[0], nest_state.shape[1])
    hidden_units = w_in.shape[1]
    nlat, nlon = lax.axis_size("lat"), lax.axis_size("lon")
    devices = nlat * nlon
    factor = 1.0 / math.sqrt(own * devices // 4 * cells)

    north, south = halo(parent, "lat", 0, False)
    west, east = halo(parent, "lon", 1, True)
    field = parent.astype(jnp.float32)
    lat_pad = jnp.concatenate([north, parent, south], axis=0).astype(jnp.float32)
    lon_pad = jnp.concatenate([west, parent, east], axis=1).astype(jnp.float32)
    beside_all = lat_pad[2:] + lat_pad[:-2] + lon_pad[:, 2:] + lon_pad[:, :-2] - 4.0 * field
    smoothed = (field + diffusion * beside_all).reshape(blat * blon, chans)
    context = jnp.take(smoothed, tile_pos, axis=0, mode="clip")
    inputs = (nest_state.astype(jnp.float32) + context[:, None, :]).astype(jnp.bfloat16)
    live = lax.iota(jnp.int32, own) < owner_count[0]
    cotangent = jnp.where(live[:, None, None], nest_cotangent, jnp.zeros_like(nest_cotangent))
    rows = inputs.reshape(own * cells, chans)
    grads = cotangent.reshape(own * cells, chans)

    total = hidden_units // BLOCK
    sizes = [total - total // 2, total // 2]
    firsts = [0, sizes[0]]
    parts, d_hidden, means = [], [], []
    for first, size in zip(firsts, sizes):
        p, dh, mean = nest_chunk(rows, grads, w_in, w_out, first, size, factor, cells)
        parts.append(p)
        d_hidden.append(dh)
        means.append(mean)

    steps = sum_steps(nlat, nlon)
    for s in range(len(steps) + len(parts) - 1):
        for k in range(len(parts)):
            if 0 <= s - k < len(steps):
                parts[k] = steps[s - k](parts[k])

    back = sum(nt(dh, w_in[:, f * BLOCK : (f + n) * BLOCK]) for dh, f, n in zip(d_hidden, firsts, sizes))
    nest_grad = (grads.astype(jnp.float32) + back).astype(jnp.bfloat16).reshape(own, cells, chans)

    lifted = sum(nn(m, w_out[f * BLOCK : (f + n) * BLOCK]) for m, f, n in zip(means, firsts, sizes))
    feedback = (jnp.mean(inputs.astype(jnp.float32), axis=1) + lifted).astype(jnp.bfloat16)
    feedback = jnp.where(live[:, None], feedback, jnp.zeros_like(feedback))
    onehot = (tile_pos[:, None] == lax.iota(jnp.int32, blat * blon)[None, :]).astype(jnp.bfloat16)
    parent_out = (smoothed + tn(onehot, feedback)).astype(jnp.bfloat16).reshape(blat, blon, chans)

    outs = ()
    for p, first in zip(parts, firsts):
        outs = widen(p, outs, first, chans, hidden_units)
    return (parent_out, nest_grad, outs[0], outs[1])


def solution(mesh):
    in_specs = (
        P("lat", "lon", None),
        P(),
        P(("lat", "lon"), None, None),
        P(("lat", "lon"), None, None),
        P(("lat", "lon")),
        P(("lat", "lon")),
        P(),
        P(),
    )
    out_specs = (P("lat", "lon", None), P(("lat", "lon"), None, None), P(), P())
    return jax.shard_map(local, mesh=mesh, in_specs=in_specs, out_specs=out_specs, check_vma=False)
```

```python
import functools
import math

import jax
import jax.numpy as jnp
from jax import lax
from jax.experimental import pallas as pl
from jax.experimental.pallas import tpu as pltpu
from jax.sharding import PartitionSpec as P

AXES = ("lat", "lon")
BLOCK = 256
GROUP = 256
LANES = 128
GELU_A = math.sqrt(2.0 / math.pi)
GELU_B = GELU_A * 0.044715

BF16, F32 = jnp.bfloat16, jnp.float32
VMEM = pl.BlockSpec(memory_space=pltpu.VMEM)
SMEM = pl.BlockSpec(memory_space=pltpu.SMEM)
ANY = pl.BlockSpec(memory_space=pl.ANY)
ORDER = "AAAAABABABABBABABFABAAFBABAFBBBBB"
TOKEN = jax.ShapeDtypeStruct((8, 128), F32)


def nn(a, b):
    return lax.dot_general(a, b, (((1,), (0,)), ((), ())), preferred_element_type=F32)


def nt(a, b):
    return lax.dot_general(a, b, (((1,), (1,)), ((), ())), preferred_element_type=F32)


def tn(a, b):
    return lax.dot_general(a, b, (((0,), (0,)), ((), ())), preferred_element_type=F32)


def shape(*dims, dtype=BF16):
    return jax.ShapeDtypeStruct(dims, dtype)


def call(kernel, name, outs, scalars, arrays, after=(), scratch=(), limit=8, flops=0, read=False):
    ins = len(scalars) + len(arrays)
    if read:
        ins += len(after)

    def body(*refs):
        kernel(*refs[:ins], *refs[ins if read else ins + len(after) :])

    moved = sum(a.size * a.dtype.itemsize for a in list(arrays) + list(outs))
    return pl.pallas_call(
        body,
        in_specs=[SMEM] * len(scalars) + [VMEM] * len(arrays) + [ANY] * len(after),
        out_specs=[VMEM] * len(outs),
        out_shape=list(outs),
        scratch_shapes=list(scratch),
        compiler_params=pltpu.CompilerParams(vmem_limit_bytes=limit << 20),
        cost_estimate=pl.CostEstimate(flops=flops, transcendentals=0, bytes_accessed=moved),
        name=name,
    )(*scalars, *arrays, *after)


def prep_kernel(count_ref, pos_ref, parent_ref, north_ref, south_ref, west_ref, east_ref, diff_ref, state_hbm, cot_hbm, flat_ref, x_ref, g_ref, state_ref, cot_ref, sems):
    blat, blon, chans = parent_ref.shape
    own, cells, _ = state_hbm.shape
    pieces = sems.shape[1]
    part = own // pieces
    copies = []
    for c in range(pieces):
        span = pl.ds(c * part, part)
        copies.append(pltpu.make_async_copy(state_hbm.at[span], state_ref.at[span], sems.at[0, c]))
        copies.append(pltpu.make_async_copy(cot_hbm.at[span], cot_ref.at[span], sems.at[1, c]))
    for copy in copies:
        copy.start()
    diffusion = diff_ref[...]
    for i in range(blat):
        here = parent_ref[i].astype(F32)
        above = (parent_ref[i - 1] if i else north_ref[0]).astype(F32)
        below = (parent_ref[i + 1] if i + 1 < blat else south_ref[0]).astype(F32)
        left = jnp.concatenate([west_ref[i].astype(F32), here[:-1]], axis=0)
        right = jnp.concatenate([here[1:], east_ref[i].astype(F32)], axis=0)
        flat_ref[i * blon : (i + 1) * blon, :] = here + diffusion * (below + above + right + left - 4.0 * here)

    def tiles(i, _):
        for u in range(8):
            t = i * 8 + u
            around = jnp.broadcast_to(flat_ref[pl.ds(pos_ref[t], 1), :], (cells, chans))
            x_ref[pl.ds(pl.multiple_of(t * cells, cells), cells), :] = (state_ref[t].astype(F32) + around).astype(BF16)
            keep = jnp.where(t < count_ref[0], 1.0, 0.0)
            g_ref[pl.ds(pl.multiple_of(t * cells, cells), cells), :] = (cot_ref[t].astype(F32) * keep).astype(BF16)
        return 0

    for c in range(pieces):
        copies[2 * c].wait()
        copies[2 * c + 1].wait()
        lax.fori_loop(c * part // 8, (c + 1) * part // 8, tiles, 0)


def row_means(values, rows_ref, cells):
    rows_ref[...] = values
    tiles = values.shape[0] // cells
    total = rows_ref[pl.ds(0, tiles, stride=cells), :]
    for r in range(1, cells):
        total = total + rows_ref[pl.ds(r, tiles, stride=cells), :]
    return total * (1.0 / cells)


def nest_kernel(first, factor, cells, meta_ref, x_ref, g_ref, win_ref, wout_ref, p_ref, dh_ref, mean_ref, act_ref, rows_ref):
    rows, chans = x_ref.shape
    tiles = GROUP // cells

    def one(j, _):
        block = pl.multiple_of(meta_ref[first + j] * BLOCK, BLOCK)
        at = pl.multiple_of(j * rows, rows)
        for i in range(rows // GROUP):
            span = slice(i * GROUP, (i + 1) * GROUP)
            hidden = nn(x_ref[span, :], win_ref[:, pl.ds(block, BLOCK)])
            d_act = nt(g_ref[span, :], wout_ref[pl.ds(block, BLOCK), :])
            square = hidden * hidden
            tanh = jnp.tanh(hidden * (GELU_A + GELU_B * square))
            cdf = 0.5 + 0.5 * tanh
            act = hidden * cdf
            slope = cdf + act * (1.0 - tanh) * (GELU_A + 3.0 * GELU_B * square)
            dh_ref[pl.ds(at + i * GROUP, GROUP), :] = (d_act * slope).astype(BF16)
            act = act.astype(BF16)
            act_ref[span, :] = act
            act = act.astype(F32)
            for l in range(BLOCK // LANES):
                lanes = slice(l * LANES, (l + 1) * LANES)
                means = row_means(act[:, lanes], rows_ref.at[i % 2, l], cells)
                mean_ref[pl.ds(pl.multiple_of(j * (rows // cells), rows // cells) + i * tiles, tiles), lanes] = means.astype(BF16)
        top = pl.multiple_of(j * 2 * chans, 2 * chans)
        out = tn(act_ref[...], g_ref[...]) * factor
        for s in range(chans // BLOCK):
            p_ref[pl.ds(top + chans + s * BLOCK, BLOCK), :] = out[:, s * BLOCK : (s + 1) * BLOCK].astype(BF16)
        p_ref[pl.ds(top, chans), :] = (tn(x_ref[...], dh_ref[pl.ds(at, rows), :]) * factor).astype(BF16)
        return 0

    one(0, 0)


def add_kernel(*refs):
    *ins, out_ref = refs
    total = ins[0][...].astype(F32)
    for ref in ins[1:]:
        total = total + ref[...].astype(F32)
    out_ref[...] = total.astype(BF16)


def split_kernel(bit, meta_ref, *refs):
    *ins, send_ref, keep_ref = refs
    half = send_ref.shape[0]
    mine = meta_ref[bit]
    for ref, which in ((send_ref, 1 - mine), (keep_ref, mine)):
        span = pl.ds(pl.multiple_of(which * half, half), half)
        total = ins[0][span, :].astype(F32)
        for part in ins[1:]:
            total = total + part[span, :].astype(F32)
        ref[...] = total.astype(BF16)


def merge_kernel(bit, meta_ref, mine_ref, got_ref, out_ref):
    half = mine_ref.shape[0]
    mine = meta_ref[bit]
    out_ref[pl.ds(pl.multiple_of(mine * half, half), half), :] = mine_ref[...]
    out_ref[pl.ds(pl.multiple_of((1 - mine) * half, half), half), :] = got_ref[...]


def widen_kernel(meta_ref, p_ref, *refs):
    gin_ref, gout_ref, token_ref = refs[-3:]
    chans, width = gin_ref.shape
    gin_ref[...] = p_ref[:chans, :].astype(F32)
    for s in range(chans // width):
        gout_ref[:, s * width : (s + 1) * width] = p_ref[chans + s * width : chans + (s + 1) * width, :].astype(F32)
    token_ref[...] = jnp.zeros_like(token_ref)


def widen(meta, slot, p, into, chans, hidden, after):
    return pl.pallas_call(
        widen_kernel,
        grid_spec=pltpu.PrefetchScalarGridSpec(
            num_scalar_prefetch=1,
            grid=(1,),
            in_specs=[VMEM] + [ANY] * (len(into) + len(after)),
            out_specs=[
                pl.BlockSpec((chans, BLOCK), lambda j, meta: (0, meta[slot])),
                pl.BlockSpec((BLOCK, chans), lambda j, meta: (meta[slot], 0)),
                VMEM,
            ],
        ),
        out_shape=[pltpu.HBM((chans, hidden), F32), pltpu.HBM((hidden, chans), F32), TOKEN],
        input_output_aliases={2 + i: i for i in range(len(into))},
        compiler_params=pltpu.CompilerParams(vmem_limit_bytes=8 << 20),
        cost_estimate=pl.CostEstimate(flops=0, transcendentals=0, bytes_accessed=12 * chans * BLOCK),
        name="widen",
    )(meta, p, *into, *after)


def back_kernel(slots, meta_ref, g_ref, win_ref, *refs):
    out_ref, token_ref = refs[-2:]
    at = pl.ds(pl.multiple_of(pl.program_id(0) * GROUP, GROUP), GROUP)
    total = g_ref[...].astype(F32)
    for slot in range(slots):
        block = pl.multiple_of(meta_ref[slot] * BLOCK, BLOCK)
        total = total + nt(refs[slot][...], win_ref[:, pl.ds(block, BLOCK)])
    out_ref[...] = total.astype(BF16)
    token_ref[...] = jnp.zeros_like(token_ref)


def back(meta, g, w_in, d_hidden, first, groups, into, after):
    rows, chans = g.shape
    slots = len(d_hidden)
    return pl.pallas_call(
        functools.partial(back_kernel, slots),
        grid=(groups,),
        in_specs=[SMEM, pl.BlockSpec((GROUP, chans), lambda j: (first + j, 0)), VMEM]
        + [pl.BlockSpec((GROUP, BLOCK), lambda j: (first + j, 0))] * slots
        + [ANY] * (len(into) + len(after)),
        out_specs=[pl.BlockSpec((GROUP, chans), lambda j: (first + j, 0)), VMEM],
        out_shape=[pltpu.HBM((rows, chans), BF16), TOKEN],
        input_output_aliases={3 + slots: 0} if into else {},
        compiler_params=pltpu.CompilerParams(vmem_limit_bytes=12 << 20),
        cost_estimate=pl.CostEstimate(
            flops=2 * groups * GROUP * chans * BLOCK * slots,
            transcendentals=0,
            bytes_accessed=2 * groups * GROUP * (2 * chans + BLOCK * slots),
        ),
        name="back",
    )(meta, g, w_in, *d_hidden, *into, *after)


def finish_kernel(count, cells, meta_ref, live_ref, x_ref, pos_ref, flat_ref, wout_ref, *refs):
    mean_refs = refs[: len(count)]
    out_ref, token_ref, own_ref, rows_ref = refs[len(count) :]
    token_ref[...] = jnp.zeros_like(token_ref)
    rows, chans = x_ref.shape
    tiles = rows // cells
    for i in range(rows // GROUP):
        wide = x_ref[i * GROUP : (i + 1) * GROUP, :].astype(F32)
        for l in range(chans // LANES):
            lanes = slice(l * LANES, (l + 1) * LANES)
            own_ref[i * (GROUP // cells) : (i + 1) * (GROUP // cells), lanes] = row_means(wide[:, lanes], rows_ref.at[l % 2], cells)
    total = own_ref[...]
    slot = 0
    for ref, n in zip(mean_refs, count):
        for j in range(n):
            block = pl.multiple_of(meta_ref[slot] * BLOCK, BLOCK)
            total = total + nn(ref[j * tiles : (j + 1) * tiles, :], wout_ref[pl.ds(block, BLOCK), :])
            slot += 1
    live = lax.broadcasted_iota(jnp.int32, total.shape, 0) < live_ref[0]
    feedback = jnp.where(live, total, 0.0).astype(BF16)
    cell = lax.broadcasted_iota(jnp.int32, (flat_ref.shape[0], tiles), 0)
    onehot = jnp.where(cell == pos_ref[...], 1.0, 0.0).astype(BF16)
    out_ref[...] = (flat_ref[...] + nn(onehot, feedback)).astype(BF16)


def halo(x, axis, dim, wrap):
    size, length = (lax.axis_size(axis), x.shape[dim])
    up = [(i, (i + 1) % size) for i in range(size if wrap else size - 1)]
    down = [(j, i) for i, j in up]
    last = lax.slice_in_dim(x, length - 1, length, axis=dim)
    first = lax.slice_in_dim(x, 0, 1, axis=dim)
    return lax.ppermute(last, axis, up), lax.ppermute(first, axis, down)


class Plan:
    def __init__(self, nlat, nlon, blocks):
        self.devices = nlat * nlon
        lon_bits = [1 << b for b in range(nlon.bit_length() - 1)]
        lat_bits = [nlon << b for b in range(nlat.bit_length() - 1)]
        self.core = lon_bits[0]
        self.near = (lat_bits[0], lon_bits[1])
        tail = lon_bits[2:] + lat_bits[1:]
        self.halved = [self.near[::-1]] + [(m, m) for m in tail[:-1]]
        self.last = (tail[-1], tail[-1])
        self.blocks = blocks

    def permute(self, x, masks):
        return lax.ppermute(x, AXES, [(i, i ^ masks[1 if i & self.core else 0]) for i in range(self.devices)])

    def meta(self):
        me = lax.axis_index(AXES)
        core = jnp.where((me & self.core) != 0, 1, 0)
        i = lax.iota(jnp.int32, self.blocks + 8)
        side = jnp.where(i % 4 >= 2, core, 1 - core)
        mask = jnp.where(side == 1, self.near[1], self.near[0])
        bit = jnp.where((me & mask) != 0, 1, 0)
        order = i // 4 * 4 + 2 * side + jnp.where(i % 2 == 1, bit, 1 - bit)
        masks = jnp.zeros_like(i)
        for s, (even, odd) in enumerate(self.halved):
            masks = jnp.where(i == self.blocks + s, jnp.where(core == 1, odd, even), masks)
        return jnp.where(i < self.blocks, order, jnp.where((me & masks) != 0, 1, 0)).astype(jnp.int32)


def local(parent, diffusion, nest_state, nest_cotangent, owner_count, tile_pos, w_in, w_out):
    blat, blon, chans = parent.shape
    own, cells = (nest_state.shape[0], nest_state.shape[1])
    rows, hidden = own * cells, w_in.shape[1]
    nlat, nlon = lax.axis_size("lat"), lax.axis_size("lon")
    factor = 1.0 / math.sqrt(own * nlat * nlon // 4 * cells)
    blocks = hidden // BLOCK
    plan = Plan(nlat, nlon, blocks)
    meta = plan.meta()

    north, south = halo(parent, "lat", 0, False)
    west, east = halo(parent, "lon", 1, True)
    flat, x, g = call(
        prep_kernel,
        "prep",
        [shape(blat * blon, chans, dtype=F32), shape(rows, chans), shape(rows, chans)],
        [owner_count, jnp.clip(tile_pos, 0, blat * blon - 1)],
        [parent, north, south, west, east, diffusion[None, :]],
        [nest_state, nest_cotangent],
        scratch=[pltpu.VMEM(nest_state.shape, BF16), pltpu.VMEM(nest_state.shape, BF16), pltpu.SemaphoreType.DMA((2, 4))],
        limit=10,
        read=True,
    )

    taken, d_hidden, means, counts = [x], [], [], []

    outs = []

    def then(value):
        taken.append(value)
        return value

    def nest(n):
        first = sum(counts)
        p, dh, mean = call(
            functools.partial(nest_kernel, first, factor, cells),
            "nest",
            [shape(n * 2 * chans, BLOCK), shape(n * rows, BLOCK), shape(n * own, BLOCK)],
            [meta],
            [x, g, w_in, w_out],
            after=taken[-1:],
            scratch=[pltpu.VMEM((rows, BLOCK), BF16), pltpu.VMEM((2, BLOCK // LANES, GROUP, LANES), F32)],
            limit=12,
            flops=8 * rows * chans * BLOCK * n,
        )
        counts.append(n)
        d_hidden.append(dh)
        means.append(mean)
        return then(p)

    def put(slot, p):
        *outs[:], token = widen(meta, slot, p, tuple(outs), chans, hidden, taken[-1:])
        taken.append(token)

    nhalf = len(plan.halved)
    pair = (plan.core, plan.core)

    def added(arrays):
        return then(call(add_kernel, "add", [shape(*arrays[0].shape)], [], arrays, taken[-1:])[0])

    def chain(k):
        slot = 4 * k
        got_send = plan.permute(nest(1), pair)
        yield
        got_keep = plan.permute(nest(1), pair)
        yield
        send = nest(1)
        yield
        near = plan.permute(added([send, got_send]), plan.near)
        yield
        parts = [nest(1), got_keep, near]
        yield
        for s, masks in enumerate(plan.halved):
            half = parts[0].shape[0] // 2
            send, keep = call(
                functools.partial(split_kernel, blocks + s), "split", [shape(half, BLOCK)] * 2, [meta], parts, taken[-1:]
            )
            parts = [keep, plan.permute(then(send), masks)]
            yield
        cur = added(parts)
        got = plan.permute(cur, plan.last)
        yield
        cur = added([cur, got])
        for s in reversed(range(nhalf)):
            got = plan.permute(cur, plan.halved[s])
            yield
            (cur,) = call(
                functools.partial(merge_kernel, blocks + s), "merge", [shape(2 * cur.shape[0], BLOCK)], [meta], [cur, got], taken[-1:]
            )
            then(cur)
        near = plan.permute(cur, plan.near)
        across = plan.permute(cur, pair)
        yield
        put(slot + 3, cur)
        yield
        put(slot + 1, across)
        yield
        across = plan.permute(near, pair)
        put(slot + 2, near)
        yield
        put(slot, across)

    results = {}

    def fillers():
        half = rows // GROUP // 2
        first, token = back(meta, g, w_in, d_hidden, 0, half, (), taken[-1:])
        then(token)
        yield
        results["back"], token = back(meta, g, w_in, d_hidden, half, rows // GROUP - half, (first,), taken[-1:])
        then(token)
        yield
        results["parent"], token = call(
            functools.partial(finish_kernel, tuple(counts), cells),
            "finish",
            [shape(blat * blon, chans), TOKEN],
            [meta, owner_count],
            [x, tile_pos[None, :], flat, w_out, *means],
            taken[-1:],
            scratch=[pltpu.VMEM((own, chans), F32), pltpu.VMEM((2, GROUP, LANES), F32)],
            flops=2 * own * chans * hidden,
        )
        then(token)

    runs = {"A": chain(0), "B": chain(1), "F": fillers()}
    for name in ORDER:
        next(runs[name], None)
    for name in "ABF":
        for _ in runs[name]:
            pass
    back_out, done = results["back"], results["parent"]
    nest_grad = back_out.reshape(own, cells, chans)
    return (done.reshape(blat, blon, chans), nest_grad, outs[0], outs[1])


def solution(mesh):
    in_specs = (
        P("lat", "lon", None),
        P(),
        P(("lat", "lon"), None, None),
        P(("lat", "lon"), None, None),
        P(("lat", "lon")),
        P(("lat", "lon")),
        P(),
        P(),
    )
    out_specs = (P("lat", "lon", None), P(("lat", "lon"), None, None), P(), P())
    return jax.shard_map(local, mesh=mesh, in_specs=in_specs, out_specs=out_specs, check_vma=False)
```
